32 devices in a mesh: groups: 2 (over y), wid: 8 (over z, x), hgt: 1, tp: 2 (over core).
Axes of the slice: x: 2, y: 2, z: 4, core: 2. Of those that a mesh axis runs over, the one named last changes fastest.
Arguments:
- self_query: bfloat16 [4, 8, 64, 2560], P('groups', 'hgt', 'wid', 'tp'), parts along dimension 0, may hold values from -250 to 250
- self_key: bfloat16 [4, 8, 64, 2560], P('groups', 'hgt', 'wid', 'tp'), parts along dimension 0, may hold values from -250 to 250
- self_value: bfloat16 [4, 8, 64, 2560], P('groups', 'hgt', 'wid', 'tp'), parts along dimension 0, may hold values from -6 to 6
- cross_query: bfloat16 [4, 8, 64, 2560], P('groups', 'hgt', 'wid', 'tp'), parts along dimension 0, may hold values from -250 to 250
- text_key: bfloat16 [1024, 2560], P(('groups', 'wid'), 'tp'), parts along dimension 0, may hold values from -25 to 25
- text_value: bfloat16 [1024, 2560], P(('groups', 'wid'), 'tp'), parts along dimension 0, may hold values from -6 to 6
- image_key: bfloat16 [514, 2560], P('groups', 'tp'), parts along dimension 0, may hold values from -25 to 25
- image_value: bfloat16 [514, 2560], P('groups', 'tp'), parts along dimension 0, may hold values from -6 to 6
- query_gain: float32 [2560], P('tp'), may hold values from 0.1 to 1.9
- key_gain: float32 [2560], P('tp'), may hold values from 0.1 to 1.9
- cross_gain: float32 [2560], P('tp'), may hold values from 0.1 to 1.9
- windows: int32 [20, 3], P('tp'), may hold values from 0 to 2, as said below
Outputs:
- self_out: bfloat16 [4, 8, 64, 2560], P('groups', 'hgt', 'wid', 'tp'), parts along dimension 0
- cross_out: bfloat16 [4, 8, 64, 2560], P('groups', 'hgt', 'wid', 'tp'), parts along dimension 0
The draws below stay inside these ranges and needn't reach their ends.
There are 2 independent parts, one for each index of `groups`. The reference program is written for one: setup_inputs(seed, part) draws one part's arguments, and reference() takes and returns one part's arrays. A program takes and returns all parts, laid end to end along the dimension named above; an argument that names none is the same for every part. Nothing has to cross between parts.
Inputs may be any that keep to these rules, and one draw needn't show every extreme that they name: windows[n] holds head n's reach in frames, in height tiles and in width tiles; the last two are 0 or 1; some head has the reach (2, 1, 1).
All inputs are finite; a program needn't handle non-finite values.
Results may differ from the reference program's by a relative error of at most 0.0081.
Values may be sent and summed in bfloat16 or wider, within the bound.
No kernel may reach another device: no remote copies, remote signals or barrier semaphores. Data moves between devices by JAX's collectives and lax.ppermute only.
A program may use at most 64 MiB of HBM per device.

```python
import math
import jax
import jax.numpy as jnp
from jax import lax

FRAMES = 2
ROWS_DEV = 8
COLS_DEV = 8
TILE = 4
FRAME_REACH = 2
HEADS = 20
HEAD_DIM = 128
TEXT_LEN = 512
IMAGE_LEN = 257
CHANNELS = 2560
HEIGHT = 8
WIDTH = 64
N_WID = 8
N_HGT = 1


def token_field(key, salt):
    base_key = jax.random.fold_in(key, salt)
    noise_key, row_key, col_key = jax.random.split(base_key, 3)
    position = jnp.arange(CHANNELS, dtype=jnp.float32) / CHANNELS
    noise = jnp.clip(jax.random.normal(noise_key, (FRAMES, HEIGHT, WIDTH, CHANNELS), jnp.float32), -4.0, 4.0)
    rising = jnp.exp(position * math.log(3.0))
    row_scale = jnp.exp(jax.random.uniform(row_key, (FRAMES, HEIGHT, WIDTH, 1), jnp.float32, 0.0, math.log(10.0)))
    rough = jnp.exp(jax.random.uniform(col_key, (CHANNELS,), jnp.float32, math.log(0.7), math.log(1.4)))
    return noise * row_scale * rising * rough


def draw_self_query(key, part):
    tokens = token_field(key, 11)
    return tokens.astype(jnp.bfloat16)


def draw_self_key(key, part):
    tokens = token_field(key, 12)
    return tokens.astype(jnp.bfloat16)


def draw_cross_query(key, part):
    tokens = token_field(key, 13)
    return tokens.astype(jnp.bfloat16)


def context_keys(key, salt, length):
    base_key = jax.random.fold_in(key, salt)
    rows_all = 2.5 * jnp.clip(jax.random.normal(base_key, (length, CHANNELS), jnp.float32), -4.0, 4.0)
    return rows_all


def draw_text_key(key, part):
    return context_keys(key, 14, TEXT_LEN).astype(jnp.bfloat16)


def draw_image_key(key, part):
    return context_keys(key, 15, IMAGE_LEN).astype(jnp.bfloat16)


def draw_windows(key, part):
    win_keys = jax.random.split(jax.random.fold_in(key, 21), 4)
    frame_win = jax.random.randint(win_keys[0], (HEADS,), 0, FRAME_REACH + 1)
    row_win = jax.random.randint(win_keys[1], (HEADS,), 0, 2)
    col_win = jax.random.randint(win_keys[2], (HEADS,), 0, 2)
    widest = jax.random.randint(win_keys[3], (), 0, HEADS)
    chosen = jnp.arange(HEADS, dtype=jnp.int32) == widest
    frame_win = jnp.where(chosen, FRAME_REACH, frame_win)
    row_win = jnp.where(chosen, 1, row_win)
    col_win = jnp.where(chosen, 1, col_win)
    return jnp.stack((frame_win, row_win, col_win), axis=1).astype(jnp.int32)


def block_scale(rng, extent, shards, smallest, largest):
    level, own = 1.0, jax.random.fold_in(rng, 6)
    for axis_at, blocks in shards:
        heights = jnp.exp(jax.random.uniform(jax.random.fold_in(own, axis_at), (blocks,), jnp.float32, smallest / len(shards), largest / len(shards)))
        level = level * jnp.repeat(heights, extent[axis_at] // blocks).reshape([-1 if axis == axis_at else 1 for axis in range(len(extent))])
    return level


def normal_values(stream_key, shape, width, limit, cuts=(), kind=jnp.bfloat16):
    array = jax.random.normal(stream_key, shape, jnp.float32) * width
    if len(cuts) > 0:
        array = block_scale(stream_key, shape, cuts, -0.22, 0.18) * array
    return jnp.clip(array, min=-limit, max=limit).astype(kind)


def setup_inputs(seed: int = 0, part: int = 0) -> dict:
    streams_of = jax.random.split(jax.random.key(seed), 13)
    part_keys = jax.random.split(jax.random.fold_in(streams_of[12], part), 13)
    self_query = draw_self_query(jax.random.fold_in(jax.random.fold_in(streams_of[12], part), 71), part)
    self_key = draw_self_key(jax.random.fold_in(jax.random.fold_in(streams_of[12], part), 71), part)
    self_value = normal_values(part_keys[2], (FRAMES, HEIGHT, WIDTH, CHANNELS), 1.0, 6.0, ((2, 8), (3, 2)))
    cross_query = draw_cross_query(jax.random.fold_in(jax.random.fold_in(streams_of[12], part), 71), part)
    text_key = draw_text_key(jax.random.fold_in(jax.random.fold_in(streams_of[12], part), 71), part)
    text_value = normal_values(part_keys[5], (TEXT_LEN, CHANNELS), 1.0, 6.0, ((0, 8), (1, 2)))
    image_key = draw_image_key(jax.random.fold_in(jax.random.fold_in(streams_of[12], part), 71), part)
    image_value = normal_values(part_keys[7], (IMAGE_LEN, CHANNELS), 1.0, 6.0, ((1, 2),))
    query_gain = jnp.clip(1.0 + 0.18 * jax.random.normal(streams_of[8], (CHANNELS,), jnp.float32), 0.1, 1.9)
    key_gain = jnp.clip(1.0 + 0.18 * jax.random.normal(streams_of[9], (CHANNELS,), jnp.float32), 0.1, 1.9)
    cross_gain = jnp.clip(1.0 + 0.18 * jax.random.normal(streams_of[10], (CHANNELS,), jnp.float32), 0.1, 1.9)
    windows = draw_windows(jax.random.fold_in(streams_of[12], 71), part)
    return {"self_query": self_query, "self_key": self_key, "self_value": self_value, "cross_query": cross_query, "text_key": text_key, "text_value": text_value, "image_key": image_key, "image_value": image_value, "query_gain": query_gain, "key_gain": key_gain, "cross_gain": cross_gain, "windows": windows}


epsilon = 1e-06
masked = -1e+30

def normalize(field, gain):
    wide = field.astype(jnp.float32)
    inverse = lax.rsqrt(lax.optimization_barrier(jnp.mean(wide * wide, axis=-1, keepdims=True)) + epsilon)
    return (wide * inverse * gain).astype(jnp.bfloat16)

def grid_positions(frame_count, row_count, col_count, row_start, col_start):
    full_shape = (frame_count, row_count, col_count)
    frame_ids = jnp.arange(frame_count, dtype=jnp.int32)[:, None, None]
    row_ids = jnp.arange(row_count, dtype=jnp.int32)[None, :, None] + row_start
    col_ids = jnp.arange(col_count, dtype=jnp.int32)[None, None, :] + col_start
    return (jnp.broadcast_to(frame_ids, full_shape).reshape(-1), jnp.broadcast_to(row_ids, full_shape).reshape(-1), jnp.broadcast_to(col_ids, full_shape).reshape(-1))

def window_mask(windows, query_pos, key_pos):
    inside = (key_pos[1] >= 0) & (key_pos[1] < HEIGHT) & (key_pos[2] >= 0) & (key_pos[2] < WIDTH)
    frame_gap = jnp.abs(query_pos[0][:, None] - key_pos[0][None, :])
    row_gap = jnp.abs(query_pos[1][:, None] // TILE - key_pos[1][None, :] // TILE)
    col_gap = jnp.abs(query_pos[2][:, None] // TILE - key_pos[2][None, :] // TILE)
    return (frame_gap[None] <= windows[:, 0, None, None]) & (row_gap[None] <= windows[:, 1, None, None]) & (col_gap[None] <= windows[:, 2, None, None]) & inside[None, None, :]

def attend(queries, key_rows, value_rows, allowed):
    factor = 1.0 / math.sqrt(HEAD_DIM)
    scores = jnp.einsum('qhd,khd->hqk', queries.astype(jnp.float32), key_rows.astype(jnp.float32)) * factor
    if allowed is not None:
        scores = jnp.where(allowed, scores, masked)
    row_top = lax.optimization_barrier(jnp.max(scores, axis=-1, keepdims=True))
    powers = jnp.exp(scores - row_top)
    if allowed is not None:
        powers = jnp.where(allowed, powers, 0.0)
    weights = lax.optimization_barrier(powers.astype(jnp.bfloat16)).astype(jnp.float32)
    numerator = jnp.einsum('hqk,khd->hqd', weights, value_rows.astype(jnp.float32))
    return numerator / lax.optimization_barrier(jnp.sum(powers, axis=-1))[..., None]

def unblock(blocks):
    shaped = blocks.reshape(N_HGT, N_WID, HEADS, FRAMES, ROWS_DEV, COLS_DEV, HEAD_DIM)
    return jnp.transpose(shaped, (3, 0, 4, 1, 5, 2, 6)).reshape(FRAMES, HEIGHT, WIDTH, CHANNELS)

def reference(self_query, self_key, self_value, cross_query, text_key, text_value, image_key, image_value, query_gain, key_gain, cross_gain, windows):
    q_normed = normalize(self_query, query_gain)
    k_normed = normalize(self_key, key_gain)
    x_normed = normalize(cross_query, cross_gain)
    margin = ((0, 0), (TILE, TILE), (TILE, TILE), (0, 0))
    k_padded = jnp.pad(k_normed, margin)
    v_padded = jnp.pad(self_value, margin)
    text_keys = text_key.reshape(TEXT_LEN, HEADS, HEAD_DIM)
    text_values = text_value.reshape(TEXT_LEN, HEADS, HEAD_DIM)
    image_keys = image_key.reshape(IMAGE_LEN, HEADS, HEAD_DIM)
    image_values = image_value.reshape(IMAGE_LEN, HEADS, HEAD_DIM)
    zero_index = jnp.zeros((), jnp.int32)
    inner_size = (FRAMES, ROWS_DEV, COLS_DEV, CHANNELS)
    outer_size = (FRAMES, ROWS_DEV + 2 * TILE, COLS_DEV + 2 * TILE, CHANNELS)

    def one_block(block_index):
        row_start = (block_index // N_WID * ROWS_DEV).astype(jnp.int32)
        col_start = (block_index % N_WID * COLS_DEV).astype(jnp.int32)
        corner = (zero_index, row_start, col_start, zero_index)
        queries = lax.dynamic_slice(q_normed, corner, inner_size).reshape(-1, HEADS, HEAD_DIM)
        crosses = lax.dynamic_slice(x_normed, corner, inner_size).reshape(-1, HEADS, HEAD_DIM)
        key_rows = lax.dynamic_slice(k_padded, corner, outer_size).reshape(-1, HEADS, HEAD_DIM)
        value_rows = lax.dynamic_slice(v_padded, corner, outer_size).reshape(-1, HEADS, HEAD_DIM)
        query_pos = grid_positions(FRAMES, ROWS_DEV, COLS_DEV, row_start, col_start)
        key_pos = grid_positions(FRAMES, ROWS_DEV + 2 * TILE, COLS_DEV + 2 * TILE, row_start - TILE, col_start - TILE)
        allowed = window_mask(windows, query_pos, key_pos)
        self_heads = attend(queries, key_rows, value_rows, allowed)
        cross_heads = attend(crosses, text_keys, text_values, None) + attend(crosses, image_keys, image_values, None)
        return (self_heads.astype(jnp.bfloat16), cross_heads.astype(jnp.bfloat16))
    self_blocks, cross_blocks = lax.map(one_block, jnp.arange(N_HGT * N_WID, dtype=jnp.int32))
    return (unblock(self_blocks), unblock(cross_blocks))
```

```python
import math

import jax
import jax.numpy as jnp
import numpy as np
from jax import lax
from jax.experimental import pallas as pl
from jax.experimental.pallas import tpu as pltpu
from jax.sharding import PartitionSpec as P

TILE = 4

epsilon = 1e-06
masked = -1e30
fields = (1, 256, 65536)
guard = 128 * sum(fields)


def on_chip():
    return pl.BlockSpec(memory_space=pltpu.VMEM)


def in_scalars():
    return pl.BlockSpec(memory_space=pltpu.SMEM)


def call(kernel, out_shapes, operands, scalars=0, **static):
    specs = [in_scalars()] * scalars + [on_chip()] * (len(operands) - scalars)

    def entry(*refs):
        kernel(refs[: len(operands)], refs[len(operands) :], **static)

    return pl.pallas_call(
        entry,
        out_shape=out_shapes,
        in_specs=specs,
        out_specs=jax.tree.map(lambda _: on_chip(), out_shapes),
        name=kernel.__name__,
    )(*operands)


def flat(value):
    return value.reshape(-1, value.shape[-1])


def square_sums(ins, outs):
    lane = lax.broadcasted_iota(jnp.int32, outs[0].shape, 1)
    total = jnp.zeros(outs[0].shape, jnp.float32)
    for place, ref in enumerate(ins):
        wide = flat(ref[...].astype(jnp.float32))
        total = jnp.where(lane == place, jnp.sum(wide * wide, axis=-1, keepdims=True), total)
    outs[0][...] = total


def inverse_of(own, other, place, channel_total):
    mean = (own[:, place : place + 1] + other[:, place : place + 1]) / channel_total
    return lax.rsqrt(mean + epsilon)


def halves(wide):
    count = wide.shape[0] // 2
    upper, lower = wide[:count], wide[count:]
    near = lax.broadcasted_iota(jnp.int32, upper.shape, 0) % (2 * TILE) < TILE
    first = jnp.where(near, upper, pltpu.roll(lower, TILE, 0))
    last = jnp.where(near, pltpu.roll(upper, count - TILE, 0), lower)
    return first, last


def normed_keys(ins, outs, channel_total):
    key, value, own, other, gain = ins
    keys_out, values_out, first_out, last_out = outs
    inverse = inverse_of(own, other, 1, channel_total)
    normed = (flat(key[...].astype(jnp.float32)) * inverse * gain[...]).astype(jnp.bfloat16)
    keys_out[...] = normed
    values = flat(value[...].astype(jnp.float32))
    values_out[...] = values.astype(jnp.bfloat16)
    for place, wide in enumerate((normed.astype(jnp.float32), values)):
        first, last = halves(wide)
        first_out[place] = first.astype(jnp.bfloat16)
        last_out[place] = last.astype(jnp.bfloat16)


def scores_of(queries, keys):
    return lax.dot_general(
        queries, keys, (((1,), (1,)), ((), ())), preferred_element_type=jnp.float32
    )


def weigh(weights, values):
    return lax.dot_general(
        weights, values, (((1,), (0,)), ((), ())), preferred_element_type=jnp.float32
    )


def self_attend(ins, outs, head_count, channel_total):
    windows, query, own, other, gain, code, beyond, keys, values, *sides = ins
    size = query.shape[-1] // head_count
    scale = math.log2(math.e) / math.sqrt(size)
    inverse = inverse_of(own, other, 0, channel_total)
    start = keys.shape[0]
    gaps = jnp.concatenate([code[:, :start], code[:, start:] + beyond[...]], 1)
    for head in range(head_count):
        cut = slice(head * size, (head + 1) * size)
        queries = flat(query[:, :, :, cut].astype(jnp.float32)) * inverse * gain[:, cut]
        rows = jnp.concatenate([keys[:, cut]] + [s[0, :, cut] for s in sides], 0)
        reach = sum(windows[head, at] * fields[at] for at in range(3)) + guard
        allowed = ((reach - gaps) & guard) == guard
        scores = scores_of(queries.astype(jnp.bfloat16), rows)
        scores = jnp.where(allowed, scores, masked)
        top = jnp.max(scores, axis=-1, keepdims=True)
        powers = jnp.exp2((scores - top) * scale)
        total = jnp.sum(powers, axis=-1, keepdims=True)
        rows = jnp.concatenate([values[:, cut]] + [s[1, :, cut] for s in sides], 0)
        result = weigh(powers.astype(jnp.bfloat16), rows) / total
        outs[0][:, :, :, cut] = result.reshape(query.shape[:-1] + (size,)).astype(jnp.bfloat16)


def image_attend(ins, outs, head_count, channel_total):
    query, own, other, gain, key, value = ins
    normed_out, part_out = outs
    size = query.shape[-1] // head_count
    scale = math.log2(math.e) / math.sqrt(size)
    inverse = inverse_of(own, other, 2, channel_total)
    bulk = key.shape[0] // 128 * 128
    for head in range(head_count):
        cut = slice(head * size, (head + 1) * size)
        queries = flat(query[:, :, :, cut].astype(jnp.float32)) * inverse * gain[:, cut]
        queries = queries.astype(jnp.bfloat16)
        normed_out[:, cut] = queries
        wide = queries.astype(jnp.float32)
        singles = []
        for row in range(bulk, key.shape[0]):
            line = key[row : row + 1, cut].astype(jnp.float32)
            singles.append(jnp.sum(wide * line, axis=-1, keepdims=True))
        top = largest(singles)
        if bulk:
            scores = scores_of(queries, key[:bulk, cut])
            most = jnp.max(scores, axis=-1, keepdims=True)
            top = most if top is None else jnp.maximum(top, most)
        total, result = 0.0, 0.0
        if bulk:
            powers = jnp.exp2((scores - top) * scale)
            total = jnp.sum(powers, axis=-1, keepdims=True)
            result = weigh(powers.astype(jnp.bfloat16), value[:bulk, cut])
        for row, single in zip(range(bulk, key.shape[0]), singles):
            power = jnp.exp2((single - top) * scale)
            total = total + power
            weight = power.astype(jnp.bfloat16).astype(jnp.float32)
            result = result + weight * value[row : row + 1, cut].astype(jnp.float32)
        part_out[:, cut] = result / total


def largest(values):
    top = None
    for value in values:
        top = value if top is None else jnp.maximum(top, value)
    return top


def text_attend(ins, outs, head_count, count):
    normed, part = ins[:2]
    keys, values = ins[2 : 2 + count], ins[2 + count :]
    size = normed.shape[-1] // head_count
    scale = math.log2(math.e) / math.sqrt(size)
    for head in range(head_count):
        cut = slice(head * size, (head + 1) * size)
        rows = jnp.concatenate([key[:, cut] for key in keys], 0)
        scores = scores_of(normed[:, cut], rows)
        top = jnp.max(scores, axis=-1, keepdims=True)
        powers = jnp.exp2((scores - top) * scale)
        total = jnp.sum(powers, axis=-1, keepdims=True)
        rows = jnp.concatenate([value[:, cut] for value in values], 0)
        result = weigh(powers.astype(jnp.bfloat16), rows) / total + part[:, cut]
        outs[0][:, :, :, cut] = result.reshape(outs[0].shape[:-1] + (size,)).astype(jnp.bfloat16)


def ring_of(count):
    order = list(range(0, count, 2)) + list(range(count - 1 - count % 2, 0, -2))
    return [(order[i], order[(i + 1) % count]) for i in range(count)]


def gather_pieces(key, value, axis):
    count = lax.axis_size(axis)
    onward = ring_of(count)
    back = [(j, i) for i, j in onward]
    keys, values = [key], [value]
    ahead, behind = (key, value), (key, value)
    for _ in range((count - 1) // 2):
        ahead = tuple(lax.ppermute(a, axis, onward) for a in ahead)
        behind = tuple(lax.ppermute(b, axis, back) for b in behind)
        keys += [ahead[0], behind[0]]
        values += [ahead[1], behind[1]]
    if count % 2 == 0:
        keys.append(lax.ppermute(ahead[0], axis, onward))
        values.append(lax.ppermute(behind[1], axis, back))
    return keys, values


def side_shift(value, axis, step):
    count = lax.axis_size(axis)
    return lax.ppermute(
        value, axis, [(i, i + step) for i in range(count) if 0 <= i + step < count]
    )


def over_pair(value, axis):
    if lax.axis_size(axis) == 2:
        return lax.ppermute(value, axis, [(0, 1), (1, 0)])
    return lax.psum(value, axis) - value


def cells(frames, rows, cols):
    grid = np.meshgrid(frames, rows, cols, indexing="ij")
    return np.stack([axis.reshape(-1) for axis in grid], 1)


def half_order(places):
    count = places.shape[0] // 2
    upper, lower = places[:count], places[count:]
    upper, lower = upper.reshape(-1, TILE, 3), lower.reshape(-1, TILE, 3)
    return np.concatenate([upper, lower], 1).reshape(-1, 3)


def gap_code(queries, keys):
    tile = lambda places: places // np.array([1, TILE, TILE])
    gaps = np.abs(tile(queries)[:, None] - tile(keys)[None])
    return (gaps * np.array(fields)).sum(-1).astype(np.int32)


def row_sides(keys, values, sides, shape, orders):
    frame_count, row_count, col_count, channels = shape
    total = frame_count * row_count * (col_count + 2 * TILE)
    wanted = cells(range(frame_count), range(row_count), range(-TILE, col_count + TILE))
    have = np.concatenate(orders, 0)
    index = {tuple(place): at for at, place in enumerate(have)}
    take = np.array([index[tuple(place)] for place in wanted])
    whole = jnp.concatenate([jnp.stack((keys, values))] + sides, 1)[:, take]
    whole = whole.reshape(2, frame_count, row_count, col_count + 2 * TILE, channels)
    above = side_shift(whole[:, :, row_count - TILE :], "hgt", 1)
    below = side_shift(whole[:, :, :TILE], "hgt", -1)
    return [side.reshape(2, -1, channels) for side in (above, below)]


def body(
    self_query,
    self_key,
    self_value,
    cross_query,
    text_key,
    text_value,
    image_key,
    image_value,
    query_gain,
    key_gain,
    cross_gain,
    windows,
):
    shape = frame_count, row_count, col_count, channels = self_query.shape
    head_count = windows.shape[0]
    channel_total = channels * lax.axis_size("tp")
    token_count = frame_count * row_count * col_count
    assert col_count == 2 * TILE and frame_count * row_count % 2 == 0
    bf16, f32 = jnp.bfloat16, jnp.float32
    gains = [gain.reshape(1, -1) for gain in (query_gain, key_gain, cross_gain)]

    text_keys, text_values = gather_pieces(text_key, text_value, "wid")

    own = call(
        square_sums,
        jax.ShapeDtypeStruct((token_count, 128), f32),
        (self_query, self_key, cross_query),
    )
    own = own[0] if isinstance(own, (list, tuple)) else own
    other = over_pair(own, "tp")
    edge = jax.ShapeDtypeStruct((2, token_count // 2, channels), bf16)
    rows = jax.ShapeDtypeStruct((token_count, channels), bf16)
    keys, values, first, last = call(
        normed_keys,
        (rows, rows, edge, edge),
        (self_key, self_value, own, other, gains[1]),
        channel_total=channel_total,
    )
    sides = [side_shift(last, "wid", 1), side_shift(first, "wid", -1)]
    frames, inner = range(frame_count), range(row_count)
    orders = [
        cells(frames, inner, range(col_count)),
        half_order(cells(frames, inner, range(-TILE, 0))),
        half_order(cells(frames, inner, range(col_count, col_count + TILE))),
    ]
    wid, hgt = lax.axis_index("wid"), lax.axis_index("hgt")
    outside = [wid == 0, wid == lax.axis_size("wid") - 1]
    if lax.axis_size("hgt") > 1:
        sides += row_sides(keys, values, sides, shape, orders)
        columns = range(-TILE, col_count + TILE)
        orders += [
            cells(frames, range(-TILE, 0), columns),
            cells(frames, range(row_count, row_count + TILE), columns),
        ]
        outside += [hgt == 0, hgt == lax.axis_size("hgt") - 1]
    places = np.concatenate(orders, 0)
    code = gap_code(orders[0], places)
    edges = [places[:, 2] < 0, places[:, 2] >= col_count, places[:, 1] < 0, places[:, 1] >= row_count]
    beyond = sum(
        jnp.asarray(edge[token_count:] * 32 * fields[2], jnp.int32) * there.astype(jnp.int32)
        for edge, there in zip(edges, outside)
    )[None]
    self_out = call(
        self_attend,
        jax.ShapeDtypeStruct(shape, bf16),
        (
            windows, self_query, own, other, gains[0], jnp.asarray(code), beyond, keys, values, *sides
        ),
        scalars=1,
        head_count=head_count,
        channel_total=channel_total,
    )
    normed, image_part = call(
        image_attend,
        (rows, jax.ShapeDtypeStruct((token_count, channels), f32)),
        (cross_query, own, other, gains[2], image_key, image_value),
        head_count=head_count,
        channel_total=channel_total,
    )
    cross_out = call(
        text_attend,
        jax.ShapeDtypeStruct(shape, bf16),
        (normed, image_part, *text_keys, *text_values),
        head_count=head_count,
        count=len(text_keys),
    )
    return (self_out, cross_out)


def solution(mesh):
    in_specs = (
        P("groups", "hgt", "wid", "tp"),
        P("groups", "hgt", "wid", "tp"),
        P("groups", "hgt", "wid", "tp"),
        P("groups", "hgt", "wid", "tp"),
        P(("groups", "wid"), "tp"),
        P(("groups", "wid"), "tp"),
        P("groups", "tp"),
        P("groups", "tp"),
        P("tp"),
        P("tp"),
        P("tp"),
        P("tp", None),
    )
    out_specs = (P("groups", "hgt", "wid", "tp"), P("groups", "hgt", "wid", "tp"))
    return jax.shard_map(body, mesh=mesh, in_specs=in_specs, out_specs=out_specs, check_vma=False)
```

```python
import math

import jax
import jax.numpy as jnp
import numpy as np
from jax import lax
from jax.experimental import pallas as pl
from jax.experimental.pallas import tpu as pltpu
from jax.sharding import PartitionSpec as P


TILE = 4
LATE = 3
KEY, QUERY, CROSS = range(3)

epsilon = 1e-06
masked = -1e30
fields = (1, 256, 65536)
guard = 128 * sum(fields)


def on_chip():
    return pl.BlockSpec(memory_space=pltpu.VMEM)


def kept(shape, dtype):
    return pltpu.VMEM(shape, dtype)


def here(value):
    return pltpu.with_memory_space_constraint(value, pltpu.VMEM)


def call(kernel, out_shapes, operands, far=(), scratch=(), **static):
    total = len(operands) + len(far)

    def entry(*refs):
        kernel(refs[:total], refs[total:], **static)

    several = isinstance(out_shapes, tuple)
    outs = out_shapes if several else (out_shapes,)
    compiled = pl.pallas_call(
        entry,
        out_shape=outs,
        in_specs=[on_chip()] * len(operands)
        + [pl.BlockSpec(memory_space=pltpu.HBM)] * len(far),
        out_specs=tuple(on_chip() for _ in outs),
        scratch_shapes=scratch,
        compiler_params=pltpu.CompilerParams(vmem_limit_bytes=16 * 2**20),
    )
    away = [pltpu.with_memory_space_constraint(value, pltpu.HBM) for value in far]
    results = compiled(*operands, *away)
    return results if several else results[0]


def loads(sources, targets, sems):
    copies = [
        pltpu.make_async_copy(source, target, sems.at[at])
        for at, (source, target) in enumerate(zip(sources, targets))
    ]
    for copy in copies:
        copy.start()
    return copies


def flat(value):
    return value.reshape(-1, value.shape[-1])


def square_sums(ins, outs):
    sums, *held, sems = outs
    copies = loads(ins, held, sems)
    lane = lax.broadcasted_iota(jnp.int32, sums.shape, 1)
    total = jnp.zeros(sums.shape, jnp.float32)
    for place, (copy, ref) in enumerate(zip(copies, held)):
        copy.wait()
        wide = flat(ref[...].astype(jnp.float32))
        total = jnp.where(lane == place, jnp.sum(wide * wide, axis=-1, keepdims=True), total)
    sums[...] = total


def inverse_of(own, other, place, channel_total):
    mean = (own[:, place : place + 1] + other[:, place : place + 1]) / channel_total
    return lax.rsqrt(mean + epsilon)


def halves(wide):
    count = wide.shape[0] // 2
    upper, lower = wide[:count], wide[count:]
    near = lax.broadcasted_iota(jnp.int32, upper.shape, 0) % (2 * TILE) < TILE
    first = jnp.where(near, upper, pltpu.roll(lower, TILE, 0))
    last = jnp.where(near, pltpu.roll(upper, count - TILE, 0), lower)
    return first, last


def normed_keys(ins, outs, channel_total, paired):
    key, own, other, gain, *sources = ins
    keys_out, values_out, *sides_out = outs[:4]
    *held, value, sems = outs[4:]
    copies = loads(sources, [value] + held, sems)
    copies[0].wait()
    odd = lax.axis_index("wid") % 2 == 1
    inverse = inverse_of(own, other, KEY, channel_total)
    for start in range(0, key.shape[-1], 128):
        cut = slice(start, start + 128)
        normed = flat(key[:, :, :, cut].astype(jnp.float32)) * inverse * gain[cut][None]
        normed = normed.astype(jnp.bfloat16)
        keys_out[:, cut] = normed
        values = flat(value[:, :, :, cut].astype(jnp.float32))
        values_out[:, cut] = values.astype(jnp.bfloat16)
        for place, wide in enumerate((normed.astype(jnp.float32), values)):
            first, last = halves(wide)
            if paired:
                first, last = jnp.where(odd, first, last), jnp.where(odd, last, first)
            sides_out[0][place, :, cut] = first.astype(jnp.bfloat16)
            sides_out[1][place, :, cut] = last.astype(jnp.bfloat16)
    for copy in copies[1:]:
        copy.wait()


def normed_queries(query, gain, inverse, cut):
    wide = flat(query[:, :, :, cut].astype(jnp.float32))
    return (wide * inverse * gain[cut][None]).astype(jnp.bfloat16)


def product(one, two, over):
    dims = (((over,), (over,)), ((), ()))
    return lax.dot_general(one, two, dims, preferred_element_type=jnp.float32)


def score(queries, keys, values, allowed=None, before=None):
    scores = product(keys, queries, 1)
    if allowed is not None:
        scores = jnp.where(allowed, scores, masked)
    top = jnp.max(scores, axis=0, keepdims=True)
    if before is not None:
        top = jnp.maximum(top, before[0])
    return scores, top, math.log2(math.e) / math.sqrt(queries.shape[-1]), values, before


def power(scores, top, scale, values, before):
    powers = jnp.exp2((scores - top) * scale)
    total = jnp.sum(powers, axis=0, keepdims=True)
    return powers.astype(jnp.bfloat16), total, top, scale, values, before


def gather(powers, total, top, scale, values, before):
    result = product(values, powers, 0)
    if before is not None:
        shrink = jnp.exp2((before[0] - top) * scale)
        total = total + before[1] * shrink
        result = result + before[2] * shrink
    return top, total, result


def attend_all(heads, together=5):
    stages = [
        lambda job: (score(**job[0]()), job[1]),
        lambda job: (power(*job[0]), job[1]),
        lambda job: (gather(*job[0]), job[1]),
        lambda job: job[1](job[0]),
    ]
    held = [heads[at : at + together] for at in range(0, len(heads), together)]
    for tick in range(len(held) + len(stages) - 1):
        for depth in reversed(range(len(stages))):
            at = tick - depth
            if 0 <= at < len(held):
                held[at] = [stages[depth](job) for job in held[at]]


def cuts(head_count, channels):
    size = channels // head_count
    return [(head, slice(head * size, (head + 1) * size)) for head in range(head_count)]


def put(out, cut, result):
    shape = out.shape[:-1] + (cut.stop - cut.start,)
    out[:, :, :, cut] = result.T.reshape(shape).astype(out.dtype)


def self_jobs(ins, outs, head_count, channel_total, paired):
    windows, query, own, other, gain, code, edges, keys, values, *sides = ins
    inverse = inverse_of(own, other, QUERY, channel_total)
    begin = keys.shape[0]
    beyond = jnp.zeros((edges.shape[0], 1), jnp.int32)
    for row, (axis, last) in enumerate((("wid", 0), ("wid", 1), ("hgt", 0), ("hgt", 1))):
        if lax.axis_size(axis) > 1 or axis == "wid":
            there = lax.axis_index(axis) == last * (lax.axis_size(axis) - 1)
            beyond = beyond + edges[:, row : row + 1] * there.astype(jnp.int32)
    outer = code[begin:] + beyond
    if paired:
        odd = lax.axis_index("wid") % 2 == 1
        half = outer.shape[0] // 2
        left, right = outer[:half], outer[half:]
        outer = jnp.concatenate([jnp.where(odd, left, right), jnp.where(odd, right, left)], 0)
    gaps = jnp.concatenate([code[:begin], outer], 0)

    def rows(place, cut):
        parts = [side[place, :, cut] for side in sides]
        if paired:
            wid, wid_count = lax.axis_index("wid"), lax.axis_size("wid")
            via = parts.pop()
            parts[1] = jnp.where((wid == 1) | (wid == wid_count - 2), via, parts[1])
        return jnp.concatenate([(keys, values)[place][:, cut]] + parts, 0)

    jobs = []
    for head, cut in cuts(head_count, query.shape[-1]):

        def start(head=head, cut=cut):
            reach = [windows[at : at + 1, head : head + 1] * fields[at] for at in range(3)]
            return dict(
                queries=normed_queries(query, gain, inverse, cut),
                keys=rows(0, cut),
                values=rows(1, cut),
                allowed=((sum(reach) + guard - gaps) & guard) == guard,
            )

        def end(merged, cut=cut):
            put(outs[0], cut, merged[2] / merged[1])

        jobs.append((start, end))
    return jobs


def image_jobs(ins, outs, head_count, inverse):
    query, _, _, gain, key, value = ins
    normed_out, part_out = outs
    jobs = []
    for _, cut in cuts(head_count, query.shape[-1]):

        def start(cut=cut):
            queries = normed_queries(query, gain, inverse, cut)
            normed_out[:, cut] = queries
            return dict(queries=queries, keys=key[:, cut], values=value[:, cut])

        def end(merged, cut=cut):
            part_out[cut, :] = merged[2] / merged[1]

        jobs.append((start, end))
    return jobs


def text_jobs(queries, keys, values, outs, head_count, channels, state=None, part=None):
    jobs = []
    for head, cut in cuts(head_count, channels):

        def start(head=head, cut=cut):
            before = None
            if state is not None:
                before = state[0][head : head + 1], state[0][16 + head : 17 + head], state[1][cut]
            return dict(
                queries=queries(cut),
                keys=jnp.concatenate([key[:, cut] for key in keys], 0),
                values=jnp.concatenate([value[:, cut] for value in values], 0),
                before=before,
            )

        def end(merged, head=head, cut=cut):
            if part is not None:
                put(outs[0], cut, merged[2] / merged[1] + part[cut, :])
            else:
                outs[0][head : head + 1] = merged[0]
                outs[0][16 + head : 17 + head] = merged[1]
                outs[1][cut, :] = merged[2]

        jobs.append((start, end))
    return jobs


def self_attend(ins, outs, **sizes):
    attend_all(self_jobs(ins, outs, **sizes))


def early_attend(ins, outs, head_count, channel_total, count):
    query, own, other, gain = ins[:4]
    inverse = inverse_of(own, other, CROSS, channel_total)
    jobs = image_jobs(ins[:6], outs[:2], head_count, inverse)
    queries = lambda cut: normed_queries(query, gain, inverse, cut)
    keys, values = ins[6 : 6 + count], ins[6 + count :]
    jobs += text_jobs(queries, keys, values, outs[2:], head_count, query.shape[-1])
    attend_all(jobs)


def text_attend(ins, outs, head_count, count):
    normed, part, *state = ins[:4]
    keys, values = ins[4 : 4 + count], ins[4 + count :]
    queries = lambda cut: normed[:, cut]
    channels = normed.shape[-1]
    attend_all(text_jobs(queries, keys, values, outs, head_count, channels, state, part))


def ring_of(count):
    order = list(range(0, count, 2)) + list(range(count - 1 - count % 2, 0, -2))
    return [(order[i], order[(i + 1) % count]) for i in range(count)]


def gather_pieces(key, value, axis):
    count = lax.axis_size(axis)
    onward = ring_of(count)
    back = [(j, i) for i, j in onward]
    keys, values = [key], [value]
    ahead, behind = [key, value], [key, value]
    for step in range(1, count // 2 + 1):
        for at, kept in enumerate((keys, values)):
            if 2 * step < count or at == 0:
                ahead[at] = lax.ppermute(ahead[at], axis, onward)
                kept.append(ahead[at])
            if 2 * step < count or at == 1:
                behind[at] = lax.ppermute(behind[at], axis, back)
                kept.append(behind[at])
    return keys, values


def side_shift(value, axis, step):
    count = lax.axis_size(axis)
    pairs = [(i, i + step) for i in range(count) if 0 <= i + step < count]
    return lax.ppermute(value, axis, pairs)


def pairs_up(wid_count, hgt_count):
    return wid_count >= 6 and wid_count % 2 == 0 and hgt_count == 1


def over_pair(value, axis):
    if lax.axis_size(axis) == 2:
        return lax.ppermute(value, axis, [(0, 1), (1, 0)])
    return lax.psum(value, axis) - value


def cells(frames, rows, cols):
    grid = np.meshgrid(frames, rows, cols, indexing="ij")
    return np.stack([axis.reshape(-1) for axis in grid], 1)


def half_order(places):
    count = places.shape[0] // 2
    upper, lower = places[:count], places[count:]
    upper, lower = upper.reshape(-1, TILE, 3), lower.reshape(-1, TILE, 3)
    return np.concatenate([upper, lower], 1).reshape(-1, 3)


def gap_code(queries, keys):
    tile = lambda places: places // np.array([1, TILE, TILE])
    gaps = np.abs(tile(queries)[:, None] - tile(keys)[None])
    return (gaps * np.array(fields)).sum(-1).astype(np.int32).T


def row_sides(keys, values, sides, shape, orders):
    frame_count, row_count, col_count, channels = shape
    wanted = cells(range(frame_count), range(row_count), range(-TILE, col_count + TILE))
    have = np.concatenate(orders, 0)
    index = {tuple(place): at for at, place in enumerate(have)}
    take = np.array([index[tuple(place)] for place in wanted])
    whole = jnp.concatenate([jnp.stack((keys, values))] + sides, 1)[:, take]
    whole = whole.reshape(2, frame_count, row_count, col_count + 2 * TILE, channels)
    above = side_shift(whole[:, :, row_count - TILE :], "hgt", 1)
    below = side_shift(whole[:, :, :TILE], "hgt", -1)
    return [side.reshape(2, -1, channels) for side in (above, below)]


def body(
    self_query,
    self_key,
    self_value,
    cross_query,
    text_key,
    text_value,
    image_key,
    image_value,
    query_gain,
    key_gain,
    cross_gain,
    windows,
):
    shape = frame_count, row_count, col_count, channels = self_query.shape
    head_count = windows.shape[0]
    channel_total = channels * lax.axis_size("tp")
    token_count = frame_count * row_count * col_count
    assert col_count == 2 * TILE and frame_count * row_count % 2 == 0
    bf16, f32 = jnp.bfloat16, jnp.float32
    gains = (query_gain, key_gain, cross_gain)

    text_keys, text_values = gather_pieces(text_key, text_value, "wid")

    raw = kept(self_query.shape, bf16)
    own, self_key, self_query, cross_query = call(
        square_sums,
        (kept((token_count, 128), f32), raw, raw, raw),
        (),
        far=(self_key, self_query, cross_query),
        scratch=(pltpu.SemaphoreType.DMA((3,)),),
    )
    self_key, self_query, cross_query = map(here, (self_key, self_query, cross_query))
    other = over_pair(own, "tp")
    border = jax.ShapeDtypeStruct((2, token_count // 2, channels), bf16)
    rows = jax.ShapeDtypeStruct((token_count, channels), bf16)
    count = lax.axis_size("wid")
    paired = pairs_up(count, lax.axis_size("hgt"))
    later = (image_key, image_value, text_key, text_value)
    keys, values, *edge_tiles = call(
        normed_keys,
        (kept(rows.shape, bf16),) * 2
        + (border, border)
        + tuple(kept(array.shape, bf16) for array in later),
        (self_key, here(own), other, gains[1]),
        far=(self_value, *later),
        scratch=(
            pltpu.VMEM(self_value.shape, bf16),
            pltpu.SemaphoreType.DMA((1 + len(later),)),
        ),
        channel_total=channel_total,
        paired=paired,
    )
    edge_tiles, later = edge_tiles[:2], list(map(here, edge_tiles[2:]))
    if paired:
        within = [(i, i ^ 1) for i in range(count)]
        across = [(i, i + i % 2 * 2 - 1) for i in range(1, count - 1)]
        away = {(2, 1): 3, (count - 3, count - 2): count - 4}
        first_leg = [(one, by) for (one, _), by in away.items()]
        second_leg = [(by, two) for (_, two), by in away.items()]
        by = lax.ppermute(edge_tiles[1], "wid", first_leg)
        sides = [
            lax.ppermute(edge_tiles[0], "wid", within),
            lax.ppermute(edge_tiles[1], "wid", [pair for pair in across if pair not in away]),
            lax.ppermute(by, "wid", second_leg),
        ]
    else:
        sides = [side_shift(edge_tiles[1], "wid", 1), side_shift(edge_tiles[0], "wid", -1)]
    frames, inner = range(frame_count), range(row_count)
    orders = [
        cells(frames, inner, range(col_count)),
        half_order(cells(frames, inner, range(-TILE, 0))),
        half_order(cells(frames, inner, range(col_count, col_count + TILE))),
    ]
    if lax.axis_size("hgt") > 1:
        sides += row_sides(keys, values, sides, shape, orders)
        columns = range(-TILE, col_count + TILE)
        orders += [
            cells(frames, range(-TILE, 0), columns),
            cells(frames, range(row_count, row_count + TILE), columns),
        ]
    places = np.concatenate(orders, 0)
    code = gap_code(orders[0], places)
    edges = [places[:, 2] < 0, places[:, 2] >= col_count, places[:, 1] < 0, places[:, 1] >= row_count]
    edges = np.stack(edges, 1)[token_count:].astype(np.int32) * (32 * fields[2])
    sizes = dict(head_count=head_count, channel_total=channel_total)
    turned = jax.ShapeDtypeStruct((channels, token_count), f32)
    result = jax.ShapeDtypeStruct(shape, bf16)
    stats = jax.ShapeDtypeStruct((32, token_count), f32)
    total = len(text_keys)
    early = max(total - LATE, 1)
    normed, image_part, *state = call(
        early_attend,
        tuple(kept(out.shape, out.dtype) for out in (rows, turned, stats, turned)),
        (cross_query, here(own), other, gains[2], *later[:3], *text_keys[1:early])
        + (later[3], *text_values[1:early]),
        count=early,
        **sizes,
    )
    operands = (windows.T, self_query, here(own), other, gains[0], jnp.asarray(code), jnp.asarray(edges))
    self_out = call(
        self_attend,
        result,
        operands + (here(keys), here(values), *sides),
        paired=paired,
        **sizes,
    )
    cross_out = call(
        text_attend,
        result,
        (*map(here, (normed, image_part, *state)), *text_keys[early:], *text_values[early:]),
        head_count=head_count,
        count=total - early,
    )
    return (self_out, cross_out)


def solution(mesh):
    in_specs = (
        P("groups", "hgt", "wid", "tp"),
        P("groups", "hgt", "wid", "tp"),
        P("groups", "hgt", "wid", "tp"),
        P("groups", "hgt", "wid", "tp"),
        P(("groups", "wid"), "tp"),
        P(("groups", "wid"), "tp"),
        P("groups", "tp"),
        P("groups", "tp"),
        P("tp"),
        P("tp"),
        P("tp"),
        P("tp", None),
    )
    out_specs = (P("groups", "hgt", "wid", "tp"), P("groups", "hgt", "wid", "tp"))

    return jax.shard_map(body, mesh=mesh, in_specs=in_specs, out_specs=out_specs, check_vma=False)
```

```python
import math

import jax
import jax.numpy as jnp
import numpy as np
from jax import lax
from jax.experimental import pallas as pl
from jax.experimental.pallas import tpu as pltpu
from jax.sharding import PartitionSpec as P


TILE = 4
LATE = 3
KEY, QUERY, CROSS = range(3)

epsilon = 1e-06
masked = -1e30
fields = (1, 256, 65536)
guard = 128 * sum(fields)


def on_chip():
    return pl.BlockSpec(memory_space=pltpu.VMEM)


def kept(shape, dtype):
    return pltpu.VMEM(shape, dtype)


def here(value):
    return pltpu.with_memory_space_constraint(value, pltpu.VMEM)


def call(kernel, out_shapes, operands, far=(), scratch=(), away=False, **static):
    total = len(operands) + len(far)

    def entry(*refs):
        kernel(refs[:total], refs[total:], **static)

    several = isinstance(out_shapes, tuple)
    outs = out_shapes if several else (out_shapes,)
    compiled = pl.pallas_call(
        entry,
        out_shape=outs,
        in_specs=[on_chip()] * len(operands)
        + [pl.BlockSpec(memory_space=pltpu.HBM)] * len(far),
        out_specs=tuple(pl.BlockSpec(memory_space=pltpu.HBM) if away else on_chip() for _ in outs),
        scratch_shapes=scratch,
        compiler_params=pltpu.CompilerParams(vmem_limit_bytes=16 * 2**20),
    )
    distant = [pltpu.with_memory_space_constraint(value, pltpu.HBM) for value in far]
    results = compiled(*operands, *distant)
    return results if several else results[0]


def loads(sources, targets, sems):
    copies = [
        pltpu.make_async_copy(source, target, sems.at[at])
        for at, (source, target) in enumerate(zip(sources, targets))
    ]
    for copy in copies:
        copy.start()
    return copies


def flat(value):
    return value.reshape(-1, value.shape[-1])


def square_sums(ins, outs):
    sums, *held, sems = outs
    copies = loads(ins, held, sems)
    lane = lax.broadcasted_iota(jnp.int32, sums.shape, 1)
    total = jnp.zeros(sums.shape, jnp.float32)
    for place, (copy, ref) in enumerate(zip(copies, held)):
        copy.wait()
        wide = flat(ref[...].astype(jnp.float32))
        total = jnp.where(lane == place, jnp.sum(wide * wide, axis=-1, keepdims=True), total)
    sums[...] = total


def inverse_of(own, other, place, channel_total):
    mean = (own[:, place : place + 1] + other[:, place : place + 1]) / channel_total
    return lax.rsqrt(mean + epsilon)


def halves(wide):
    count = wide.shape[0] // 2
    upper, lower = wide[:count], wide[count:]
    near = lax.broadcasted_iota(jnp.int32, upper.shape, 0) % (2 * TILE) < TILE
    first = jnp.where(near, upper, pltpu.roll(lower, TILE, 0))
    last = jnp.where(near, pltpu.roll(upper, count - TILE, 0), lower)
    return first, last


def normed_keys(ins, outs, channel_total, paired):
    key, own, other, gain, windows, *sources = ins
    keys_out, values_out, *sides_out = outs[:4]
    reach_out, *held, value, sems = outs[4:]
    copies = loads(sources, [value] + held, sems)
    for head in range(reach_out.shape[0]):
        reach = [windows[at : at + 1, head : head + 1] * fields[at] for at in range(3)]
        reach_out[head : head + 1, :] = jnp.broadcast_to(sum(reach) + guard, (1, reach_out.shape[1]))
    copies[0].wait()
    odd = lax.axis_index("wid") % 2 == 1
    inverse = inverse_of(own, other, KEY, channel_total)
    for start in range(0, key.shape[-1], 128):
        cut = slice(start, start + 128)
        normed = flat(key[:, :, :, cut].astype(jnp.float32)) * inverse * gain[cut][None]
        normed = normed.astype(jnp.bfloat16)
        keys_out[:, cut] = normed
        values = flat(value[:, :, :, cut].astype(jnp.float32))
        values_out[:, cut] = values.astype(jnp.bfloat16)
        for place, wide in enumerate((normed.astype(jnp.float32), values)):
            first, last = halves(wide)
            if paired:
                first, last = jnp.where(odd, first, last), jnp.where(odd, last, first)
            sides_out[0][place, :, cut] = first.astype(jnp.bfloat16)
            sides_out[1][place, :, cut] = last.astype(jnp.bfloat16)
    for copy in copies[1:]:
        copy.wait()


def normed_queries(query, gain, inverse, cut):
    wide = flat(query[:, :, :, cut].astype(jnp.float32))
    return (wide * inverse * gain[cut][None]).astype(jnp.bfloat16)


def product(one, two, over):
    dims = (((over,), (over,)), ((), ()))
    return lax.dot_general(one, two, dims, preferred_element_type=jnp.float32)


def score(queries, keys, values, shift=None, before=None):
    scores = product(keys, queries, 1)
    if shift is not None:
        scores = scores + shift
    top = jnp.max(scores, axis=0, keepdims=True)
    if before is not None:
        top = jnp.maximum(top, before[0])
    return scores, top, math.log2(math.e) / math.sqrt(queries.shape[-1]), values, before


def power(scores, top, scale, values, before):
    powers = jnp.exp2((scores - top) * scale)
    total = jnp.sum(powers, axis=0, keepdims=True)
    return powers.astype(jnp.bfloat16), total, top, scale, values, before


def gather(powers, total, top, scale, values, before):
    result = product(values, powers, 0)
    if before is not None:
        shrink = jnp.exp2((before[0] - top) * scale)
        total = total + before[1] * shrink
        result = result + before[2] * shrink
    return top, total, result


def attend_all(heads, together=5):
    stages = [
        lambda job: (score(**job[0]()), job[1]),
        lambda job: (power(*job[0]), job[1]),
        lambda job: (gather(*job[0]), job[1]),
        lambda job: job[1](job[0]),
    ]
    held = [heads[at : at + together] for at in range(0, len(heads), together)]
    for tick in range(len(held) + len(stages) - 1):
        for depth in reversed(range(len(stages))):
            at = tick - depth
            if 0 <= at < len(held):
                held[at] = [stages[depth](job) for job in held[at]]


def cuts(head_count, channels):
    size = channels // head_count
    return [(head, slice(head * size, (head + 1) * size)) for head in range(head_count)]


class Outgoing:
    def __init__(self, target, held, sems):
        self.target, self.held, self.sems, self.copies = target, held, sems, []

    def put(self, cut, result):
        shape = self.held.shape[:-1] + (cut.stop - cut.start,)
        place = (slice(None),) * 3 + (cut,)
        self.held[place] = result.T.reshape(shape).astype(self.held.dtype)
        sem = self.sems.at[len(self.copies)]
        copy = pltpu.make_async_copy(self.held.at[place], self.target.at[place], sem)
        copy.start()
        self.copies.append(copy)

    def wait(self):
        for copy in self.copies:
            copy.wait()


def self_jobs(ins, outs, head_count, channel_total, paired, repeat):
    reach, query, own, other, gain, code, edges, keys, values, *sides = ins
    inverse = inverse_of(own, other, QUERY, channel_total)
    begin = keys.shape[0]
    beyond = jnp.zeros((edges.shape[0], 1), jnp.int32)
    for row, (axis, last) in enumerate((("wid", 0), ("wid", 1), ("hgt", 0), ("hgt", 1))):
        if lax.axis_size(axis) > 1 or axis == "wid":
            there = lax.axis_index(axis) == last * (lax.axis_size(axis) - 1)
            beyond = beyond + edges[:, row : row + 1] * there.astype(jnp.int32)
    own_count = begin // repeat
    outer = code[own_count:] + beyond
    if paired:
        odd = lax.axis_index("wid") % 2 == 1
        half = outer.shape[0] // 2
        left, right = outer[:half], outer[half:]
        outer = jnp.concatenate([jnp.where(odd, left, right), jnp.where(odd, right, left)], 0)
    gaps = jnp.concatenate([code[:own_count], outer], 0)

    def spread(values):
        groups = values.reshape(-1, 1, 2 * TILE, values.shape[-1])
        groups = jnp.broadcast_to(groups, (groups.shape[0], repeat) + groups.shape[2:])
        return groups.reshape(-1, values.shape[-1])

    def rows(place, cut):
        parts = [side[place, :, cut] for side in sides]
        if paired:
            wid, wid_count = lax.axis_index("wid"), lax.axis_size("wid")
            via = parts.pop()
            parts[1] = jnp.where((wid == 1) | (wid == wid_count - 2), via, parts[1])
        return jnp.concatenate([(keys, values)[place][:, cut]] + parts, 0)

    jobs = []
    for head, cut in cuts(head_count, query.shape[-1]):

        def start(head=head, cut=cut):
            return dict(
                queries=normed_queries(query, gain, inverse, cut),
                keys=rows(0, cut),
                values=rows(1, cut),
                shift=spread(
                    jnp.where(((reach[head : head + 1] - gaps) & guard) == guard, 0.0, masked)
                ),
            )

        def end(merged, cut=cut):
            outs[0].put(cut, merged[2] / merged[1])

        jobs.append((start, end))
    return jobs


def image_jobs(ins, outs, head_count, inverse):
    query, _, _, gain, key, value = ins
    normed_out, part_out = outs
    jobs = []
    for _, cut in cuts(head_count, query.shape[-1]):

        def start(cut=cut):
            queries = normed_queries(query, gain, inverse, cut)
            normed_out[:, cut] = queries
            return dict(queries=queries, keys=key[:, cut], values=value[:, cut])

        def end(merged, cut=cut):
            part_out[cut, :] = merged[2] / merged[1]

        jobs.append((start, end))
    return jobs


def text_jobs(queries, keys, values, outs, head_count, channels, state=None, part=None):
    jobs = []
    for head, cut in cuts(head_count, channels):

        def start(head=head, cut=cut):
            before = None
            if state is not None:
                before = state[0][head : head + 1], state[0][16 + head : 17 + head], state[1][cut]
            return dict(
                queries=queries(cut),
                keys=jnp.concatenate([key[:, cut] for key in keys], 0),
                values=jnp.concatenate([value[:, cut] for value in values], 0),
                before=before,
            )

        def end(merged, head=head, cut=cut):
            if part is not None:
                outs[0].put(cut, merged[2] / merged[1] + part[cut, :])
            else:
                outs[0][head : head + 1] = merged[0]
                outs[0][16 + head : 17 + head] = merged[1]
                outs[1][cut, :] = merged[2]

        jobs.append((start, end))
    return jobs


def self_attend(ins, outs, **sizes):
    out = Outgoing(*outs)
    attend_all(self_jobs(ins, [out], **sizes))
    out.wait()


def early_attend(ins, outs, head_count, channel_total, count):
    query, own, other, gain = ins[:4]
    inverse = inverse_of(own, other, CROSS, channel_total)
    jobs = image_jobs(ins[:6], outs[:2], head_count, inverse)
    queries = lambda cut: normed_queries(query, gain, inverse, cut)
    keys, values = ins[6 : 6 + count], ins[6 + count :]
    jobs += text_jobs(queries, keys, values, outs[2:], head_count, query.shape[-1])
    attend_all(jobs)


def text_attend(ins, outs, head_count, count):
    normed, part, *state = ins[:4]
    keys, values = ins[4 : 4 + count], ins[4 + count :]
    queries = lambda cut: normed[:, cut]
    channels = normed.shape[-1]
    out = Outgoing(*outs)
    attend_all(text_jobs(queries, keys, values, [out], head_count, channels, state, part))
    out.wait()


def ring_of(count):
    order = list(range(0, count, 2)) + list(range(count - 1 - count % 2, 0, -2))
    return [(order[i], order[(i + 1) % count]) for i in range(count)]


def gather_pieces(key, value, axis):
    count = lax.axis_size(axis)
    onward = ring_of(count)
    back = [(j, i) for i, j in onward]
    keys, values = [key], [value]
    ahead, behind = [key, value], [key, value]
    for step in range(1, count // 2 + 1):
        for at, kept in enumerate((keys, values)):
            if 2 * step < count or at == 0:
                ahead[at] = send(ahead[at], axis, onward)
                kept.append(ahead[at])
            if 2 * step < count or at == 1:
                behind[at] = send(behind[at], axis, back)
                kept.append(behind[at])
    return keys, values


def send(value, axis, pairs):
    return lax.ppermute(value, axis, pairs)


def filled(pairs, count):
    busy = {place for pair in pairs for place in pair}
    return pairs + [(place, place) for place in range(count) if place not in busy]


def side_shift(value, axis, step):
    count = lax.axis_size(axis)
    pairs = [(i, i + step) for i in range(count) if 0 <= i + step < count]
    return send(value, axis, pairs)


def pairs_up(wid_count, hgt_count):
    return wid_count >= 6 and wid_count % 2 == 0 and hgt_count == 1


def over_pair(value, axis):
    if lax.axis_size(axis) == 2:
        return send(value, axis, [(0, 1), (1, 0)])
    return lax.psum(value, axis) - value


def cells(frames, rows, cols):
    grid = np.meshgrid(frames, rows, cols, indexing="ij")
    return np.stack([axis.reshape(-1) for axis in grid], 1)


def half_order(places):
    count = places.shape[0] // 2
    upper, lower = places[:count], places[count:]
    upper, lower = upper.reshape(-1, TILE, 3), lower.reshape(-1, TILE, 3)
    return np.concatenate([upper, lower], 1).reshape(-1, 3)


def gap_code(queries, keys):
    tile = lambda places: places // np.array([1, TILE, TILE])
    gaps = np.abs(tile(queries)[:, None] - tile(keys)[None])
    return (gaps * np.array(fields)).sum(-1).astype(np.int32).T


def thinned(*tables):
    split = [table.reshape(-1, TILE, 2 * TILE, table.shape[-1]) for table in tables]
    if all((table == table[:, :1]).all() for table in split):
        return TILE, *(table[:, 0].reshape(-1, table.shape[-1]) for table in split)
    return 1, *tables


def row_sides(keys, values, sides, shape, orders):
    frame_count, row_count, col_count, channels = shape
    wanted = cells(range(frame_count), range(row_count), range(-TILE, col_count + TILE))
    have = np.concatenate(orders, 0)
    index = {tuple(place): at for at, place in enumerate(have)}
    take = np.array([index[tuple(place)] for place in wanted])
    whole = jnp.concatenate([jnp.stack((keys, values))] + sides, 1)[:, take]
    whole = whole.reshape(2, frame_count, row_count, col_count + 2 * TILE, channels)
    above = side_shift(whole[:, :, row_count - TILE :], "hgt", 1)
    below = side_shift(whole[:, :, :TILE], "hgt", -1)
    return [side.reshape(2, -1, channels) for side in (above, below)]


def body(
    self_query,
    self_key,
    self_value,
    cross_query,
    text_key,
    text_value,
    image_key,
    image_value,
    query_gain,
    key_gain,
    cross_gain,
    windows,
):
    shape = frame_count, row_count, col_count, channels = self_query.shape
    head_count = windows.shape[0]
    channel_total = channels * lax.axis_size("tp")
    token_count = frame_count * row_count * col_count
    assert col_count == 2 * TILE and frame_count * row_count % 2 == 0
    bf16, f32 = jnp.bfloat16, jnp.float32
    gains = (query_gain, key_gain, cross_gain)

    text_keys, text_values = gather_pieces(text_key, text_value, "wid")

    raw = kept(self_query.shape, bf16)
    own, self_key, self_query, cross_query = call(
        square_sums,
        (kept((token_count, 128), f32), raw, raw, raw),
        (),
        far=(self_key, self_query, cross_query),
        scratch=(pltpu.SemaphoreType.DMA((3,)),),
    )
    self_key, self_query, cross_query = map(here, (self_key, self_query, cross_query))
    other = over_pair(own, "tp")
    border = jax.ShapeDtypeStruct((2, token_count // 2, channels), bf16)
    rows = jax.ShapeDtypeStruct((token_count, channels), bf16)
    count = lax.axis_size("wid")
    paired = pairs_up(count, lax.axis_size("hgt"))
    later = (image_key, image_value, text_key, text_value)
    keys, values, *edge_tiles = call(
        normed_keys,
        (kept(rows.shape, bf16),) * 2
        + (border, border, kept((head_count, token_count), jnp.int32))
        + tuple(kept(array.shape, bf16) for array in later),
        (self_key, here(own), other, gains[1], windows.T),
        far=(self_value, *later),
        scratch=(
            pltpu.VMEM(self_value.shape, bf16),
            pltpu.SemaphoreType.DMA((1 + len(later),)),
        ),
        channel_total=channel_total,
        paired=paired,
    )
    edge_tiles, reach, later = edge_tiles[:2], here(edge_tiles[2]), list(map(here, edge_tiles[3:]))
    if paired:
        within = [(i, i ^ 1) for i in range(count)]
        across = [(i, i + i % 2 * 2 - 1) for i in range(1, count - 1)]
        away = {(2, 1): 3, (count - 3, count - 2): count - 4}
        first_leg = [(one, by) for (one, _), by in away.items()]
        second_leg = [(by, two) for (_, two), by in away.items()]
        both_ways = first_leg + [(two, one) for one, two in first_leg]
        by = send(edge_tiles[1], "wid", filled(both_ways, count))
        sides = [
            send(edge_tiles[0], "wid", within),
            send(edge_tiles[1], "wid", filled([pair for pair in across if pair not in away], count)),
            send(by, "wid", filled(second_leg, count)),
        ]
    else:
        sides = [side_shift(edge_tiles[1], "wid", 1), side_shift(edge_tiles[0], "wid", -1)]
    frames, inner = range(frame_count), range(row_count)
    orders = [
        cells(frames, inner, range(col_count)),
        half_order(cells(frames, inner, range(-TILE, 0))),
        half_order(cells(frames, inner, range(col_count, col_count + TILE))),
    ]
    if lax.axis_size("hgt") > 1:
        sides += row_sides(keys, values, sides, shape, orders)
        columns = range(-TILE, col_count + TILE)
        orders += [
            cells(frames, range(-TILE, 0), columns),
            cells(frames, range(row_count, row_count + TILE), columns),
        ]
    places = np.concatenate(orders, 0)
    code = gap_code(orders[0], places)
    edges = [places[:, 2] < 0, places[:, 2] >= col_count, places[:, 1] < 0, places[:, 1] >= row_count]
    edges = np.stack(edges, 1)[token_count:].astype(np.int32) * (32 * fields[2])
    repeat, code, edges = thinned(code, edges)
    sizes = dict(head_count=head_count, channel_total=channel_total)
    turned = jax.ShapeDtypeStruct((channels, token_count), f32)
    result = jax.ShapeDtypeStruct(shape, bf16)
    stats = jax.ShapeDtypeStruct((32, token_count), f32)
    total = len(text_keys)
    early = max(total - LATE, 1)
    normed, image_part, *state = call(
        early_attend,
        tuple(kept(out.shape, out.dtype) for out in (rows, turned, stats, turned)),
        (cross_query, here(own), other, gains[2], *later[:3], *text_keys[1:early])
        + (later[3], *text_values[1:early]),
        count=early,
        **sizes,
    )
    operands = (reach, self_query, here(own), other, gains[0], jnp.asarray(code), jnp.asarray(edges))
    sending = dict(
        away=True,
        scratch=(pltpu.VMEM(shape, bf16), pltpu.SemaphoreType.DMA((head_count,))),
    )
    self_out = call(
        self_attend,
        result,
        operands + (here(keys), here(values), *sides),
        paired=paired,
        repeat=repeat,
        **sending,
        **sizes,
    )
    cross_out = call(
        text_attend,
        result,
        (*map(here, (normed, image_part, *state)), *text_keys[early:], *text_values[early:]),
        head_count=head_count,
        count=total - early,
        **sending,
    )
    return (self_out, cross_out)


def solution(mesh):
    in_specs = (
        P("groups", "hgt", "wid", "tp"),
        P("groups", "hgt", "wid", "tp"),
        P("groups", "hgt", "wid", "tp"),
        P("groups", "hgt", "wid", "tp"),
        P(("groups", "wid"), "tp"),
        P(("groups", "wid"), "tp"),
        P("groups", "tp"),
        P("groups", "tp"),
        P("tp"),
        P("tp"),
        P("tp"),
        P("tp", None),
    )
    out_specs = (P("groups", "hgt", "wid", "tp"), P("groups", "hgt", "wid", "tp"))

    return jax.shard_map(body, mesh=mesh, in_specs=in_specs, out_specs=out_specs, check_vma=False)
```

```python
import math

import jax
import jax.numpy as jnp
import numpy as np
from jax import lax
from jax.experimental import pallas as pl
from jax.experimental.pallas import tpu as pltpu
from jax.sharding import PartitionSpec as P


TILE = 4
LATE = 3
KEY, QUERY, CROSS = range(3)

epsilon = 1e-06
masked = -1e30
fields = (1, 256, 65536)
guard = 128 * sum(fields)


def on_chip():
    return pl.BlockSpec(memory_space=pltpu.VMEM)


def kept(shape, dtype):
    return pltpu.VMEM(shape, dtype)


def here(value):
    return pltpu.with_memory_space_constraint(value, pltpu.VMEM)


def call(kernel, out_shapes, operands, far=(), scratch=(), away=0, **static):
    total = len(operands) + len(far)

    def entry(*refs):
        kernel(refs[:total], refs[total:], **static)

    several = isinstance(out_shapes, tuple)
    outs = out_shapes if several else (out_shapes,)
    compiled = pl.pallas_call(
        entry,
        out_shape=outs,
        in_specs=[on_chip()] * len(operands)
        + [pl.BlockSpec(memory_space=pltpu.HBM)] * len(far),
        out_specs=tuple(
            pl.BlockSpec(memory_space=pltpu.HBM) if at < away else on_chip()
            for at in range(len(outs))
        ),
        scratch_shapes=scratch,
        compiler_params=pltpu.CompilerParams(vmem_limit_bytes=16 * 2**20),
    )
    distant = [pltpu.with_memory_space_constraint(value, pltpu.HBM) for value in far]
    results = compiled(*operands, *distant)
    return results if several else results[0]


def loads(sources, targets, sems):
    copies = [
        pltpu.make_async_copy(source, target, sems.at[at])
        for at, (source, target) in enumerate(zip(sources, targets))
    ]
    for copy in copies:
        copy.start()
    return copies


def flat(value):
    return value.reshape(-1, value.shape[-1])


def square_sums(ins, outs):
    sums, *held, sems = outs
    copies = loads(ins, held, sems)
    lane = lax.broadcasted_iota(jnp.int32, sums.shape, 1)
    total = jnp.zeros(sums.shape, jnp.float32)
    for place, (copy, ref) in enumerate(zip(copies, held)):
        copy.wait()
        wide = flat(ref[...].astype(jnp.float32))
        total = jnp.where(lane == place, jnp.sum(wide * wide, axis=-1, keepdims=True), total)
    sums[...] = total


def inverse_of(own, other, place, channel_total):
    mean = (own[:, place : place + 1] + other[:, place : place + 1]) / channel_total
    return lax.rsqrt(mean + epsilon)


def halves(wide):
    count = wide.shape[0] // 2
    upper, lower = wide[:count], wide[count:]
    near = lax.broadcasted_iota(jnp.int32, upper.shape, 0) % (2 * TILE) < TILE
    first = jnp.where(near, upper, pltpu.roll(lower, TILE, 0))
    last = jnp.where(near, pltpu.roll(upper, count - TILE, 0), lower)
    return first, last


def normed_keys(ins, outs, channel_total, paired):
    key, own, other, gain, windows, *sources = ins
    keys_out, values_out, *sides_out = outs[:4]
    reach_out, *held, value, sems = outs[4:]
    copies = loads(sources, [value] + held, sems)
    for head in range(reach_out.shape[0]):
        reach = [windows[at : at + 1, head : head + 1] * fields[at] for at in range(3)]
        reach_out[head : head + 1, :] = jnp.broadcast_to(sum(reach) + guard, (1, reach_out.shape[1]))
    copies[0].wait()
    odd = lax.axis_index("wid") % 2 == 1
    inverse = inverse_of(own, other, KEY, channel_total)
    for start in range(0, key.shape[-1], 128):
        cut = slice(start, start + 128)
        normed = flat(key[:, :, :, cut].astype(jnp.float32)) * inverse * gain[cut][None]
        normed = normed.astype(jnp.bfloat16)
        keys_out[:, cut] = normed
        values = flat(value[:, :, :, cut].astype(jnp.float32))
        values_out[:, cut] = values.astype(jnp.bfloat16)
        for place, wide in enumerate((normed.astype(jnp.float32), values)):
            first, last = halves(wide)
            if paired:
                first, last = jnp.where(odd, first, last), jnp.where(odd, last, first)
            sides_out[0][place, :, cut] = first.astype(jnp.bfloat16)
            sides_out[1][place, :, cut] = last.astype(jnp.bfloat16)
    for copy in copies[1:]:
        copy.wait()


def normed_queries(query, gain, inverse, cut):
    wide = flat(query[:, :, :, cut].astype(jnp.float32))
    return (wide * inverse * gain[cut][None]).astype(jnp.bfloat16)


def product(one, two, over):
    dims = (((over,), (over,)), ((), ()))
    return lax.dot_general(one, two, dims, preferred_element_type=jnp.float32)


def score(queries, keys, values, shift=None, before=None):
    scores = product(keys, queries, 1)
    if shift is not None:
        scores = scores + shift
    top = jnp.max(scores, axis=0, keepdims=True)
    if before is not None:
        top = jnp.maximum(top, before[0])
    return scores, top, math.log2(math.e) / math.sqrt(queries.shape[-1]), values, before


def power(scores, top, scale, values, before):
    powers = jnp.exp2((scores - top) * scale)
    total = jnp.sum(powers, axis=0, keepdims=True)
    return powers.astype(jnp.bfloat16), total, top, scale, values, before


def gather(powers, total, top, scale, values, before):
    result = product(values, powers, 0)
    if before is not None:
        shrink = jnp.exp2((before[0] - top) * scale)
        total = total + before[1] * shrink
        result = result + before[2] * shrink
    return top, total, result


def attend_all(heads, together=5):
    stages = [
        lambda job: (score(**job[0]()), job[1]),
        lambda job: (power(*job[0]), job[1]),
        lambda job: (gather(*job[0]), job[1]),
        lambda job: job[1](job[0]),
    ]
    held = [heads[at : at + together] for at in range(0, len(heads), together)]
    for tick in range(len(held) + len(stages) - 1):
        for depth in reversed(range(len(stages))):
            at = tick - depth
            if 0 <= at < len(held):
                held[at] = [stages[depth](job) for job in held[at]]


def cuts(head_count, channels):
    size = channels // head_count
    return [(head, slice(head * size, (head + 1) * size)) for head in range(head_count)]


class Outgoing:
    def __init__(self, target, held, sems):
        self.target, self.held, self.sems, self.copies = target, held, sems, []

    def put(self, cut, result):
        shape = self.held.shape[:-1] + (cut.stop - cut.start,)
        place = (slice(None),) * 3 + (cut,)
        self.held[place] = result.T.reshape(shape).astype(self.held.dtype)
        sem = self.sems.at[len(self.copies)]
        copy = pltpu.make_async_copy(self.held.at[place], self.target.at[place], sem)
        copy.start()
        self.copies.append(copy)

    def wait(self):
        for copy in self.copies:
            copy.wait()


def self_jobs(ins, outs, head_count, channel_total, paired, repeat):
    reach, query, own, other, gain, code, edges, keys, values, *sides = ins
    inverse = inverse_of(own, other, QUERY, channel_total)
    begin = keys.shape[0]
    beyond = jnp.zeros((edges.shape[0], 1), jnp.int32)
    for row, (axis, last) in enumerate((("wid", 0), ("wid", 1), ("hgt", 0), ("hgt", 1))):
        if lax.axis_size(axis) > 1 or axis == "wid":
            there = lax.axis_index(axis) == last * (lax.axis_size(axis) - 1)
            beyond = beyond + edges[:, row : row + 1] * there.astype(jnp.int32)
    own_count = begin // repeat
    outer = code[own_count:] + beyond
    if paired:
        odd = lax.axis_index("wid") % 2 == 1
        half = outer.shape[0] // 2
        left, right = outer[:half], outer[half:]
        outer = jnp.concatenate([jnp.where(odd, left, right), jnp.where(odd, right, left)], 0)
    gaps = jnp.concatenate([code[:own_count], outer], 0)

    def spread(values):
        groups = values.reshape(-1, 1, 2 * TILE, values.shape[-1])
        groups = jnp.broadcast_to(groups, (groups.shape[0], repeat) + groups.shape[2:])
        return groups.reshape(-1, values.shape[-1])

    def rows(place, cut):
        parts = [side[place, :, cut] for side in sides]
        if paired:
            wid, wid_count = lax.axis_index("wid"), lax.axis_size("wid")
            via = parts.pop()
            parts[1] = jnp.where((wid == 1) | (wid == wid_count - 2), via, parts[1])
        return jnp.concatenate([(keys, values)[place][:, cut]] + parts, 0)

    jobs = []
    for head, cut in cuts(head_count, query.shape[-1]):

        def start(head=head, cut=cut):
            return dict(
                queries=normed_queries(query, gain, inverse, cut),
                keys=rows(0, cut),
                values=rows(1, cut),
                shift=spread(
                    jnp.where(((reach[head : head + 1] - gaps) & guard) == guard, 0.0, masked)
                ),
            )

        def end(merged, cut=cut):
            outs[0].put(cut, merged[2] / merged[1])

        jobs.append((start, end))
    return jobs


def image_jobs(ins, outs, head_count, inverse):
    query, _, _, gain, key, value = ins
    normed_out, part_out = outs
    jobs = []
    for _, cut in cuts(head_count, query.shape[-1]):

        def start(cut=cut):
            queries = normed_queries(query, gain, inverse, cut)
            normed_out[:, cut] = queries
            return dict(queries=queries, keys=key[:, cut], values=value[:, cut])

        def end(merged, cut=cut):
            part_out[cut, :] = merged[2] / merged[1]

        jobs.append((start, end))
    return jobs


def text_jobs(queries, keys, values, outs, head_count, channels, state=None, part=None):
    jobs = []
    for head, cut in cuts(head_count, channels):

        def start(head=head, cut=cut):
            before = None
            if state is not None:
                before = state[0][head : head + 1], state[0][16 + head : 17 + head], state[1][cut]
            return dict(
                queries=queries(cut),
                keys=jnp.concatenate([key[:, cut] for key in keys], 0),
                values=jnp.concatenate([value[:, cut] for value in values], 0),
                before=before,
            )

        def end(merged, head=head, cut=cut):
            if part is not None:
                outs[0].put(cut, merged[2] / merged[1] + part[cut, :])
            else:
                outs[0][head : head + 1] = merged[0]
                outs[0][16 + head : 17 + head] = merged[1]
                outs[1][cut, :] = merged[2]

        jobs.append((start, end))
    return jobs


def self_attend(ins, outs, head_count, count, **sizes):
    own, (normed, *state), texts = ins[: -3 - 2 * count], ins[-3 - 2 * count :][:3], ins[-2 * count :]
    target, *later, held, sems = outs
    out = Outgoing(target, held, sems)
    queries = lambda cut: normed[:, cut]
    channels = normed.shape[-1]
    jobs = text_jobs(queries, texts[:count], texts[count:], later, head_count, channels, state)
    attend_all(jobs + self_jobs(own, [out], head_count, **sizes))
    out.wait()


def early_attend(ins, outs, head_count, channel_total, count):
    query, own, other, gain = ins[:4]
    *results, key, value, image_key, image_value, sems = outs
    copies = loads(ins[-4:], (key, value, image_key, image_value), sems)
    inverse = inverse_of(own, other, CROSS, channel_total)
    queries = lambda cut: normed_queries(query, gain, inverse, cut)
    keys, values = [key, *ins[4 : 3 + count]], [value, *ins[3 + count : -4]]
    texts = text_jobs(queries, keys, values, results[2:], head_count, query.shape[-1])
    images = image_jobs((*ins[:4], image_key, image_value), results[:2], head_count, inverse)
    attend_all([after(copies[:2], texts[0])] + texts[1:] + [after(copies[2:], images[0])] + images[1:])


def after(copies, job):
    def start():
        for copy in copies:
            copy.wait()
        return job[0]()

    return start, job[1]


def text_attend(ins, outs, head_count, count):
    normed, part, *state = ins[:4]
    keys, values = ins[4 : 4 + count], ins[4 + count :]
    queries = lambda cut: normed[:, cut]
    channels = normed.shape[-1]
    out = Outgoing(*outs)
    attend_all(text_jobs(queries, keys, values, [out], head_count, channels, state, part))
    out.wait()


def ring_of(count):
    order = list(range(0, count, 2)) + list(range(count - 1 - count % 2, 0, -2))
    return [(order[i], order[(i + 1) % count]) for i in range(count)]


def gather_pieces(key, value, axis):
    count = lax.axis_size(axis)
    onward = ring_of(count)
    back = [(j, i) for i, j in onward]
    keys, values = [key], [value]
    ahead, behind = [key, value], [key, value]
    for step in range(1, count // 2 + 1):
        for at, kept in enumerate((keys, values)):
            if 2 * step < count or at == 0:
                ahead[at] = send(ahead[at], axis, onward)
                kept.append(ahead[at])
            if 2 * step < count or at == 1:
                behind[at] = send(behind[at], axis, back)
                kept.append(behind[at])
    return keys, values


def send(value, axis, pairs):
    return lax.ppermute(value, axis, pairs)


def in_every_group(pairs, count):
    total = lax.axis_size("groups") * count
    busy = {one for one, _ in pairs}
    pairs = [(start + one, start + two) for start in range(0, total, count) for one, two in pairs]
    return pairs + [(i, (i + count) % total) for i in range(total) if i % count not in busy]


def filled(pairs, count):
    busy = {place for pair in pairs for place in pair}
    return pairs + [(place, place) for place in range(count) if place not in busy]


def side_shift(value, axis, step):
    count = lax.axis_size(axis)
    pairs = [(i, i + step) for i in range(count) if 0 <= i + step < count]
    return send(value, axis, pairs)


def pairs_up(wid_count, hgt_count):
    return wid_count >= 6 and wid_count % 2 == 0 and hgt_count == 1


def over_pair(value, axis):
    if lax.axis_size(axis) == 2:
        return send(value, axis, [(0, 1), (1, 0)])
    return lax.psum(value, axis) - value


def cells(frames, rows, cols):
    grid = np.meshgrid(frames, rows, cols, indexing="ij")
    return np.stack([axis.reshape(-1) for axis in grid], 1)


def half_order(places):
    count = places.shape[0] // 2
    upper, lower = places[:count], places[count:]
    upper, lower = upper.reshape(-1, TILE, 3), lower.reshape(-1, TILE, 3)
    return np.concatenate([upper, lower], 1).reshape(-1, 3)


def gap_code(queries, keys):
    tile = lambda places: places // np.array([1, TILE, TILE])
    gaps = np.abs(tile(queries)[:, None] - tile(keys)[None])
    return (gaps * np.array(fields)).sum(-1).astype(np.int32).T


def thinned(*tables):
    split = [table.reshape(-1, TILE, 2 * TILE, table.shape[-1]) for table in tables]
    if all((table == table[:, :1]).all() for table in split):
        return TILE, *(table[:, 0].reshape(-1, table.shape[-1]) for table in split)
    return 1, *tables


def row_sides(keys, values, sides, shape, orders):
    frame_count, row_count, col_count, channels = shape
    wanted = cells(range(frame_count), range(row_count), range(-TILE, col_count + TILE))
    have = np.concatenate(orders, 0)
    index = {tuple(place): at for at, place in enumerate(have)}
    take = np.array([index[tuple(place)] for place in wanted])
    whole = jnp.concatenate([jnp.stack((keys, values))] + sides, 1)[:, take]
    whole = whole.reshape(2, frame_count, row_count, col_count + 2 * TILE, channels)
    above = side_shift(whole[:, :, row_count - TILE :], "hgt", 1)
    below = side_shift(whole[:, :, :TILE], "hgt", -1)
    return [side.reshape(2, -1, channels) for side in (above, below)]


def body(
    self_query,
    self_key,
    self_value,
    cross_query,
    text_key,
    text_value,
    image_key,
    image_value,
    query_gain,
    key_gain,
    cross_gain,
    windows,
):
    shape = frame_count, row_count, col_count, channels = self_query.shape
    head_count = windows.shape[0]
    channel_total = channels * lax.axis_size("tp")
    token_count = frame_count * row_count * col_count
    assert col_count == 2 * TILE and frame_count * row_count % 2 == 0
    bf16, f32 = jnp.bfloat16, jnp.float32
    gains = (query_gain, key_gain, cross_gain)

    text_keys, text_values = gather_pieces(text_key, text_value, "wid")

    raw = kept(self_query.shape, bf16)
    own, self_key, self_query, cross_query = call(
        square_sums,
        (kept((token_count, 128), f32), raw, raw, raw),
        (),
        far=(self_key, self_query, cross_query),
        scratch=(pltpu.SemaphoreType.DMA((3,)),),
    )
    self_key, self_query, cross_query = map(here, (self_key, self_query, cross_query))
    other = over_pair(own, "tp")
    border = jax.ShapeDtypeStruct((2, token_count // 2, channels), bf16)
    rows = jax.ShapeDtypeStruct((token_count, channels), bf16)
    count = lax.axis_size("wid")
    paired = pairs_up(count, lax.axis_size("hgt"))
    keys, values, *edge_tiles = call(
        normed_keys,
        (kept(rows.shape, bf16),) * 2
        + (border, border, kept((head_count, token_count), jnp.int32)),
        (self_key, here(own), other, gains[1], windows.T),
        far=(self_value,),
        scratch=(
            pltpu.VMEM(self_value.shape, bf16),
            pltpu.SemaphoreType.DMA((1,)),
        ),
        channel_total=channel_total,
        paired=paired,
    )
    edge_tiles, reach = edge_tiles[:2], here(edge_tiles[2])
    if paired:
        within = [(i, i ^ 1) for i in range(count)]
        across = [(i, i + i % 2 * 2 - 1) for i in range(1, count - 1)]
        away = {(2, 1): 3, (count - 3, count - 2): count - 4}
        first_leg = [(one, by) for (one, _), by in away.items()]
        second_leg = [(by, two) for (_, two), by in away.items()]
        both_ways = first_leg + [(two, one) for one, two in first_leg]
        by = send(edge_tiles[1], ("groups", "wid"), in_every_group(both_ways, count))
        sides = [
            send(edge_tiles[0], "wid", within),
            send(edge_tiles[1], "wid", filled([pair for pair in across if pair not in away], count)),
            send(by, "wid", filled(second_leg, count)),
        ]
    else:
        sides = [side_shift(edge_tiles[1], "wid", 1), side_shift(edge_tiles[0], "wid", -1)]
    frames, inner = range(frame_count), range(row_count)
    orders = [
        cells(frames, inner, range(col_count)),
        half_order(cells(frames, inner, range(-TILE, 0))),
        half_order(cells(frames, inner, range(col_count, col_count + TILE))),
    ]
    if lax.axis_size("hgt") > 1:
        sides += row_sides(keys, values, sides, shape, orders)
        columns = range(-TILE, col_count + TILE)
        orders += [
            cells(frames, range(-TILE, 0), columns),
            cells(frames, range(row_count, row_count + TILE), columns),
        ]
    places = np.concatenate(orders, 0)
    code = gap_code(orders[0], places)
    edges = [places[:, 2] < 0, places[:, 2] >= col_count, places[:, 1] < 0, places[:, 1] >= row_count]
    edges = np.stack(edges, 1)[token_count:].astype(np.int32) * (32 * fields[2])
    repeat, code, edges = thinned(code, edges)
    sizes = dict(head_count=head_count, channel_total=channel_total)
    turned = jax.ShapeDtypeStruct((channels, token_count), f32)
    result = jax.ShapeDtypeStruct(shape, bf16)
    stats = jax.ShapeDtypeStruct((32, token_count), f32)
    total = len(text_keys)
    early = max(total - LATE, 1)
    normed, image_part, *state = call(
        early_attend,
        tuple(kept(out.shape, out.dtype) for out in (rows, turned, stats, turned)),
        (cross_query, here(own), other, gains[2], *text_keys[1:early])
        + (*text_values[1:early],),
        far=(text_key, text_value, image_key, image_value),
        scratch=(
            pltpu.VMEM(text_key.shape, bf16),
            pltpu.VMEM(text_value.shape, bf16),
            pltpu.VMEM(image_key.shape, bf16),
            pltpu.VMEM(image_value.shape, bf16),
            pltpu.SemaphoreType.DMA((4,)),
        ),
        count=early,
        **sizes,
    )
    operands = (reach, self_query, here(own), other, gains[0], jnp.asarray(code), jnp.asarray(edges))
    sending = dict(
        away=1,
        scratch=(pltpu.VMEM(shape, bf16), pltpu.SemaphoreType.DMA((head_count,))),
    )
    late = total - 1
    middle = (*text_keys[early:late], *text_values[early:late])
    normed = here(normed)
    self_out, *state = call(
        self_attend,
        (result, kept(stats.shape, f32), kept(turned.shape, f32)),
        operands + (here(keys), here(values), *sides, normed, *map(here, state), *middle),
        count=late - early,
        paired=paired,
        repeat=repeat,
        **sending,
        **sizes,
    )
    cross_out = call(
        text_attend,
        result,
        (normed, here(image_part), *map(here, state), *text_keys[late:], *text_values[late:]),
        head_count=head_count,
        count=total - late,
        **sending,
    )
    return (self_out, cross_out)


def solution(mesh):
    in_specs = (
        P("groups", "hgt", "wid", "tp"),
        P("groups", "hgt", "wid", "tp"),
        P("groups", "hgt", "wid", "tp"),
        P("groups", "hgt", "wid", "tp"),
        P(("groups", "wid"), "tp"),
        P(("groups", "wid"), "tp"),
        P("groups", "tp"),
        P("groups", "tp"),
        P("tp"),
        P("tp"),
        P("tp"),
        P("tp", None),
    )
    out_specs = (P("groups", "hgt", "wid", "tp"), P("groups", "hgt", "wid", "tp"))

    return jax.shard_map(body, mesh=mesh, in_specs=in_specs, out_specs=out_specs, check_vma=False)
```
